32 devices in a mesh: dom: 8 (over z, y), tm: 4 (over x, core).
Axes of the slice: x: 2, y: 2, z: 4, core: 2. Of those that a mesh axis runs over, the one named last changes fastest.
Arguments:
- panel_signal: bfloat16 [8, 8192], P('tm', 'dom'), may hold values from -6 to 6
- panel_box: int32 [8192], P('dom'), may hold values from 0 to 15
- radiation: bfloat16 [8192, 1024], P('dom'), may hold values from -0.75 to 0.75
- reception: bfloat16 [8192, 1024], P('dom'), may hold values from -0.1875 to 0.1875
- translation: bfloat16 [64, 8, 1024], P(None, None, 'dom'), may hold values from -1 to 1
- list_source: int32 [128, 8], replicated, may hold values from 0 to 127
- list_class: int32 [128, 8], replicated, may hold values from 0 to 63
- list_count: int32 [128], replicated, may hold values from 1 to 8, as said below
Outputs:
- panel_field: bfloat16 [8, 8192], P('tm', 'dom')
The draws below stay inside these ranges and needn't reach their ends.
Inputs may be any that keep to these rules, and one draw needn't show every extreme that they name: `panel_box`: indices a panel's box among the 16 boxes of its own index of dom. Box a uses the first list_count[a] entries of its lists; the rest are padding.
All inputs are finite; a program needn't handle non-finite values.
Results may differ from the reference program's by a relative error of at most 0.0057.
Values may be sent and summed in bfloat16 or wider, within the bound.
A program may use at most 64 MiB of HBM per device.

```python
import math
import jax
import jax.numpy as jnp
import numpy as np
from jax import lax

K = 1024
PAN_DEV = 1024
BOX_DEV = 16
J = 8
C = 64
TS = 8
B = 128
PAN = 8192
N_DOM = 8


def draw_list_count(key, part):
    counts = jax.random.randint(jax.random.fold_in(key, 7), (B,), 1, J + 1)
    return counts.at[0].set(J).astype(jnp.int32)


def with_ends(values, key, low, largest):
    spot = [jax.random.randint(jax.random.fold_in(key, axis), (), 0, length) for axis, length in enumerate(values.shape)]
    widest = values.shape.index(max(values.shape))
    next_to = spot[:widest] + [(spot[widest] + 1) % values.shape[widest]] + spot[widest + 1:]
    return values.at[tuple(spot)].set(low).at[tuple(next_to)].set(largest)


def levels(rng, shape, cuts, least, largest):
    def one(dim, parts):
        steps = jax.random.uniform(jax.random.fold_in(jax.random.fold_in(rng, 6), dim), (parts,), jnp.float32, least / len(cuts), largest / len(cuts))
        return jnp.repeat(jnp.exp(steps), shape[dim] // parts).reshape((-1,) + (1,) * (len(shape) - dim - 1))

    factor_of = one(*cuts[0])
    for cut in cuts[1:]:
        factor_of = factor_of * one(*cut)
    return factor_of


def rank_table(number_of, skew):
    portions = [(1 << 20) // math.isqrt(standing ** skew) + 1 for standing in range(1, number_of + 1)]
    spread = 1 + sum(portions) // (1 << 30)
    return np.cumsum(np.array([max(1, weight // spread) for weight in portions]))


def ranked(own_key, extent, count, lean):
    table = rank_table(count, lean)
    pick = jax.random.randint(jax.random.fold_in(own_key, 1), extent, 0, int(table[count - 1]))
    grade = jnp.searchsorted(jnp.asarray(table, jnp.int32), pick, side="right")
    return jax.random.permutation(jax.random.fold_in(own_key, 2), count)[grade].astype(jnp.int32)


def gaussian(key, dims, scale, limit, shards=(), kind=jnp.bfloat16):
    drawn = jax.random.normal(key, dims, jnp.float32) * scale
    if len(shards) > 0:
        drawn = levels(key, dims, shards, -0.22, 0.18) * drawn
    return jnp.clip(drawn, min=-limit, max=limit).astype(kind)


def setup_inputs(seed: int = 0) -> dict:
    key_of = jax.random.split(jax.random.key(seed), 9)
    panel_signal = gaussian(key_of[0], (TS, PAN), 1.0, 6.0, ((0, 4), (1, 8)))
    panel_box = with_ends(ranked(key_of[1], (PAN,), BOX_DEV, 2), jax.random.fold_in(key_of[1], 3), 0, BOX_DEV - 1).astype(jnp.int32)
    radiation = gaussian(key_of[2], (PAN, K), (PAN_DEV // BOX_DEV) ** -0.5, 0.75, ((0, 8),))
    reception = gaussian(key_of[3], (PAN, K), K ** -0.5, 0.1875, ((0, 8),))
    translation = gaussian(key_of[4], (C, TS, K), (J * TS // 2) ** -0.5, 1.0, ((2, 8),))
    list_source = with_ends(jax.random.randint(key_of[5], (B, J), 0, B), jax.random.fold_in(key_of[5], 1), 0, B - 1).astype(jnp.int32)
    list_class = with_ends(jax.random.randint(key_of[6], (B, J), 0, C), jax.random.fold_in(key_of[6], 1), 0, C - 1).astype(jnp.int32)
    list_count = draw_list_count(jax.random.fold_in(key_of[8], 71), 0)
    return {"panel_signal": panel_signal, "panel_box": panel_box, "radiation": radiation, "reception": reception, "translation": translation, "list_source": list_source, "list_class": list_class, "list_count": list_count}


def aggregate_block(signal, owner, weights):
    count_rows = signal.shape[0]
    box_onehot = (owner[None, :] == jnp.arange(BOX_DEV, dtype=jnp.int32)[:, None]).astype(signal.dtype)
    masked = (signal[:, None, :] * box_onehot[None]).reshape(count_rows * BOX_DEV, PAN_DEV)
    summed = jnp.dot(masked, weights, preferred_element_type=jnp.float32)
    return summed.astype(jnp.bfloat16).reshape(count_rows, BOX_DEV, K)


def reference(panel_signal, panel_box, radiation, reception, translation, list_source, list_class, list_count):
    def outgoing_block(index):
        signal = lax.dynamic_slice_in_dim(panel_signal, index * PAN_DEV, PAN_DEV, 1)
        owner = lax.dynamic_slice_in_dim(panel_box, index * PAN_DEV, PAN_DEV, 0)
        weights = lax.dynamic_slice_in_dim(radiation, index * PAN_DEV, PAN_DEV, 0)
        return aggregate_block(signal, owner, weights)

    outgoing = lax.map(outgoing_block, jnp.arange(N_DOM, dtype=jnp.int32))
    outgoing = jnp.transpose(outgoing, (1, 0, 2, 3)).reshape(TS, B, K)
    used = (jnp.arange(J, dtype=jnp.int32)[None, :] < list_count[:, None])

    def direction_block(index):
        first = index * 32
        rays = lax.dynamic_slice_in_dim(outgoing, first, 32, 2)
        kernel = lax.dynamic_slice_in_dim(translation, first, 32, 2)
        lag_kernel = jnp.transpose(kernel, (1, 0, 2))[:, list_class, :] * used[None, :, :, None].astype(kernel.dtype)
        gathered = rays[:, list_source, :]
        result = []
        for step_out in range(TS):
            total = jnp.zeros((B, 32), jnp.float32)
            for step_in in range(step_out + 1):
                total = total + jnp.sum(lag_kernel[step_out - step_in].astype(jnp.float32) * gathered[step_in].astype(jnp.float32), axis=1)
            result.append(total.astype(jnp.bfloat16))
        return jnp.stack(result)

    incoming = lax.map(direction_block, jnp.arange(K // 32, dtype=jnp.int32))
    incoming = jnp.transpose(incoming, (1, 2, 0, 3)).reshape(TS, B, K)

    def field_block(index):
        rays = lax.dynamic_slice_in_dim(incoming, index * BOX_DEV, BOX_DEV, 1)
        owner = lax.dynamic_slice_in_dim(panel_box, index * PAN_DEV, PAN_DEV, 0)
        weights = lax.dynamic_slice_in_dim(reception, index * PAN_DEV, PAN_DEV, 0)
        partial_value = lax.dot_general(rays.reshape(TS * BOX_DEV, K), weights, (((1,), (1,)), ((), ())), preferred_element_type=jnp.float32)
        partial_value = partial_value.reshape(TS, BOX_DEV, PAN_DEV)
        box_onehot = (owner[None, :] == jnp.arange(BOX_DEV, dtype=jnp.int32)[:, None]).astype(jnp.float32)
        return jnp.sum(partial_value * box_onehot[None], axis=1).astype(jnp.bfloat16)

    field = lax.map(field_block, jnp.arange(N_DOM, dtype=jnp.int32))
    return jnp.transpose(field, (1, 0, 2)).reshape(TS, PAN)
```

```python
import functools
import math

import jax
import jax.numpy as jnp
from jax import lax
from jax.experimental import pallas as pl
from jax.experimental.pallas import tpu as pltpu
from jax.sharding import PartitionSpec as P

def lag_sum(kern_rows, gathered, out_steps, offset):
    entries = kern_rows.shape[0]
    lags_all = kern_rows.shape[1]
    width = kern_rows.shape[2]
    results = []
    for step_out in range(out_steps):
        total = jnp.zeros((entries, width), jnp.float32)
        for step_in in range(gathered.shape[1]):
            delay = offset + step_out - step_in
            picked = lax.dynamic_index_in_dim(
                kern_rows, jnp.clip(delay, 0, lags_all - 1), 1, keepdims=False
            )
            weight = jnp.where(delay >= 0, picked.astype(jnp.float32), 0.0)
            total = total + weight * gathered[:, step_in].astype(jnp.float32)
        results.append(total)
    return jnp.stack(results, axis=1)


def body(
    panel_signal, panel_box, radiation, reception, translation, list_source, list_class, list_count
):
    rows_own = panel_signal.shape[0]
    dirs_own = translation.shape[2]
    boxes_all = list_source.shape[0]
    classes_all = translation.shape[0]
    lags_all = translation.shape[1]
    BOX_DEV = boxes_all // lax.axis_size("dom")
    J = list_source.shape[1]
    box_onehot = (panel_box[None, :] == jnp.arange(BOX_DEV, dtype=jnp.int32)[:, None]).astype(
        jnp.bfloat16
    )
    used_rows = (jnp.arange(J, dtype=jnp.int32)[None, :] < list_count[:, None]).astype(jnp.bfloat16)
    block_size = math.gcd(boxes_all, 256)

    def translate_all(table, rays, out_steps, offset):
        width = table.shape[2]
        count_in = rays.shape[1]
        flat_table = table.reshape(classes_all, lags_all * width)
        flat_rays = rays.reshape(boxes_all, count_in * width)

        def one_block(index):
            sources = lax.dynamic_slice_in_dim(
                list_source, index * block_size, block_size, 0
            ).reshape(block_size * J)
            classes = lax.dynamic_slice_in_dim(
                list_class, index * block_size, block_size, 0
            ).reshape(block_size * J)
            keep_rows = lax.dynamic_slice_in_dim(
                used_rows, index * block_size, block_size, 0
            ).reshape(block_size * J, 1)
            kern_rows = (jnp.take(flat_table, classes, axis=0) * keep_rows).reshape(
                block_size * J, lags_all, width
            )
            gathered = jnp.take(flat_rays, sources, axis=0).reshape(block_size * J, count_in, width)
            summed = lag_sum(kern_rows, gathered, out_steps, offset)
            return jnp.sum(summed.reshape(block_size, J, out_steps, width), axis=1)

        blocks = lax.map(one_block, jnp.arange(boxes_all // block_size, dtype=jnp.int32))
        return blocks.reshape(boxes_all, out_steps, width)

    masked = panel_signal[:, None, :] * box_onehot[None]
    outgoing = jnp.einsum(
        "rbp,pk->brk", masked, radiation, preferred_element_type=jnp.float32
    ).astype(jnp.bfloat16)
    spread = lax.all_to_all(outgoing, "dom", split_axis=2, concat_axis=0, tiled=True)
    first = lax.axis_index("tm") * rows_own
    empty = jnp.zeros((boxes_all, rows_own, dirs_own), jnp.float32)
    piece = lax.all_gather(spread, "tm", axis=1, tiled=True)

    def active():
        return empty + translate_all(translation, piece, rows_own, first)

    def passive():
        return empty

    incoming = lax.cond(jnp.int32(0) <= first + rows_own - 1, active, passive)
    rays = lax.all_to_all(
        incoming.astype(jnp.bfloat16), "dom", split_axis=0, concat_axis=2, tiled=True
    )
    partial_value = jnp.einsum("brk,pk->brp", rays, reception, preferred_element_type=jnp.float32)
    field = jnp.sum(partial_value * box_onehot.astype(jnp.float32)[:, None, :], axis=0)
    return field.astype(jnp.bfloat16)


LANES = 128
SUBLANES = 8
MESH = pl.DeviceIdType.MESH


def pick_lanes(parts, lane_group):
    total = parts[0]
    for index in range(1, len(parts)):
        total = jnp.where(lane_group == index, parts[index], total)
    return total


def spin(values, shift):
    shift = shift % LANES
    return values if shift == 0 else pltpu.roll(values, shift, 1)


def kernel(
    n_dom,
    n_tm,
    signal_ref,
    box_ref,
    rad_hbm,
    rec_hbm,
    trans_hbm,
    source_ref,
    class_ref,
    count_ref,
    out_ref,
    rad,
    rec,
    trans,
    trans_wide,
    kern,
    rays,
    send_out,
    recv_out,
    send_in,
    recv_in,
    rows_tmp,
    load_sem,
    out_send_sem,
    out_recv_sem,
    in_send_sem,
    in_recv_sem,
):
    n_dev = n_dom * n_tm
    dom, tm = lax.axis_index("dom"), lax.axis_index("tm")
    me = dom * n_tm + tm
    steps_own, panels = signal_ref.shape
    dirs_all = rad.shape[1]
    classes, lags, _ = trans.shape
    entries = source_ref.shape[0]
    boxes_own = source_ref.shape[1] // n_dom
    span = LANES // n_tm
    pieces = boxes_own // n_tm
    block = steps_own * pieces
    rows_all = n_tm * block
    halves = lags // n_tm
    chunks = load_sem.shape[0] // 2 - 1
    depth = panels // chunks

    def place(peer):
        return {"dom": lax.div(peer, n_tm), "tm": lax.rem(peer, n_tm)}

    def rad_copy(index):
        at = pl.ds(index * depth, depth)
        return pltpu.make_async_copy(rad_hbm.at[at, :], rad.at[at, :], load_sem.at[index])

    rec_copy = pltpu.make_async_copy(rec_hbm, rec, load_sem.at[chunks])
    trans_copy = pltpu.make_async_copy(trans_hbm, trans, load_sem.at[chunks + 1])

    for index in range(chunks):
        rad_copy(index).start()
    trans_copy.start()
    rec_copy.start()

    barrier = pltpu.get_barrier_semaphore()

    def greet(offset, carry):
        peer = lax.rem(me + offset, n_dev)
        pl.semaphore_signal(barrier, inc=1, device_id=place(peer), device_id_type=MESH)
        return carry

    lax.fori_loop(1, n_dev, greet, 0)

    lane_group = lax.broadcasted_iota(jnp.int32, (SUBLANES, LANES), 1) // span
    sublane = lax.broadcasted_iota(jnp.int32, (SUBLANES, LANES), 0)

    row = lax.broadcasted_iota(jnp.int32, (rows_all, panels), 0)
    row_box = (row % pieces) * n_tm + row // block
    owned = box_ref[...] == row_box
    signal = signal_ref[...].astype(jnp.float32)
    spread = signal[0:1]
    row_step = (row // pieces) % steps_own
    for step in range(1, steps_own):
        spread = jnp.where(row_step == step, signal[step : step + 1], spread)
    masked = jnp.where(owned, spread, 0.0).astype(jnp.bfloat16)

    outgoing = jnp.zeros((rows_all, dirs_all), jnp.float32)
    for index in range(chunks):
        rad_copy(index).wait()
        outgoing = outgoing + jnp.dot(
            masked[:, index * depth : (index + 1) * depth],
            rad[index * depth : (index + 1) * depth, :],
            preferred_element_type=jnp.float32,
        )
    for owner in range(n_dom):
        tiles = [
            outgoing[part * block : (part + 1) * block, owner * LANES : (owner + 1) * LANES]
            for part in range(n_tm)
        ]
        for time in range(n_tm):
            moved = [spin(tiles[part], span * (part - time)) for part in range(n_tm)]
            send_out[owner * n_tm + time] = pick_lanes(moved, lane_group).astype(jnp.bfloat16)

    pl.semaphore_wait(barrier, n_dev - 1)

    def out_copy(peer, slot):
        return pltpu.make_async_remote_copy(
            src_ref=send_out.at[peer],
            dst_ref=recv_out.at[slot],
            send_sem=out_send_sem.at[peer],
            recv_sem=out_recv_sem.at[slot],
            device_id=place(peer),
            device_id_type=MESH,
        )

    def in_copy(peer, slot):
        return pltpu.make_async_remote_copy(
            src_ref=send_in.at[peer],
            dst_ref=recv_in.at[slot],
            send_sem=in_send_sem.at[peer],
            recv_sem=in_recv_sem.at[slot],
            device_id=place(peer),
            device_id_type=MESH,
        )

    def send_first(offset, carry):
        out_copy(lax.rem(me + offset, n_dev), me).start()
        return carry

    lax.fori_loop(1, n_dev, send_first, 0)
    recv_out[me] = send_out[me]

    trans_copy.wait()
    trans_wide[...] = trans[...].astype(jnp.float32).reshape(classes * lags, LANES)
    kern[classes] = jnp.zeros((halves, SUBLANES, LANES), jnp.float32)

    def spread_class(index, carry):
        base = index * (SUBLANES * lags)
        for half in range(halves):
            moved = []
            for part in range(n_tm):
                tile = trans_wide[pl.ds(base + half * n_tm + part, SUBLANES, stride=lags), :]
                shift = lax.rem((part - tm + n_tm) * span, LANES)
                moved.append(pltpu.roll(tile, shift, 1))
            tile = pick_lanes(moved, lane_group)
            for at in range(SUBLANES):
                kern[index * SUBLANES + at, half] = jnp.broadcast_to(
                    tile[at : at + 1], (SUBLANES, LANES)
                )
        return carry

    lax.fori_loop(0, classes // SUBLANES, spread_class, 0)

    def take_rays(step, carry):
        owner = lax.rem(dom + step, n_dom)
        for time in range(n_tm):
            slot = owner * n_tm + time

            @pl.when(slot != me)
            def _():
                out_copy(slot, slot).wait_recv()

            rows_tmp[time * block : (time + 1) * block, :] = recv_out[slot].astype(jnp.float32)
        for piece in range(pieces):
            tile = rows_tmp[pl.ds(piece, SUBLANES, stride=pieces), :]
            later = [tile]
            for lag in range(1, n_tm):
                later.append(jnp.where(sublane >= lag, pltpu.roll(tile, lag, 0), 0.0))
            for part in range(n_tm):
                moved = [spin(later[lag], span * (lag - part)) for lag in range(n_tm)]
                rays[owner * boxes_own + piece * n_tm + part] = pick_lanes(moved, lane_group)
        return carry

    lax.fori_loop(0, n_dom, take_rays, 0)

    def translate(step, carry):
        owner = lax.rem(dom + step, n_dom)

        def one_piece(piece, inner):
            sums = []
            for part in range(n_tm):
                box = owner * boxes_own + piece * n_tm + part
                used = count_ref[box]
                totals = [jnp.zeros((SUBLANES, LANES), jnp.float32) for _ in range(halves)]
                for entry in range(entries):
                    kind = jnp.where(entry < used, class_ref[entry, box], classes)
                    ray = rays[source_ref[entry, box]]
                    for half in range(halves):
                        totals[half] = totals[half] + kern[kind, half] * ray
                total = totals[0]
                for half in range(1, halves):
                    late = half * n_tm
                    total = total + jnp.where(
                        sublane >= late, pltpu.roll(totals[half], late, 0), 0.0
                    )
                turn = LANES // 2
                while turn >= span:
                    total = total + pltpu.roll(total, turn, 1)
                    turn //= 2
                sums.append(total)
            rows_tmp[pl.ds(piece, SUBLANES, stride=pieces), :] = pick_lanes(sums, lane_group)
            return inner

        lax.fori_loop(0, pieces, one_piece, 0)
        for time in range(n_tm):
            slot = owner * n_tm + time
            send_in[slot] = rows_tmp[time * block : (time + 1) * block, :].astype(jnp.bfloat16)

            @pl.when(slot != me)
            def _():
                in_copy(slot, me).start()

        return carry

    lax.fori_loop(1, n_dom + 1, translate, 0)
    recv_in[me] = send_in[me]

    rec_copy.wait()
    field = jnp.zeros((rows_all, panels), jnp.float32)
    for owner in range(n_dom):
        tiles = []
        for time in range(n_tm):
            slot = owner * n_tm + time

            @pl.when(slot != me)
            def _():
                in_copy(slot, slot).wait_recv()

            tiles.append(recv_in[slot].astype(jnp.float32))
        incoming = []
        for part in range(n_tm):
            moved = [spin(tiles[time], span * (time - part)) for time in range(n_tm)]
            incoming.append(pick_lanes(moved, lane_group))
        incoming = jnp.concatenate(incoming, axis=0).astype(jnp.bfloat16)
        field = field + lax.dot_general(
            incoming,
            rec[:, owner * LANES : (owner + 1) * LANES],
            (((1,), (1,)), ((), ())),
            preferred_element_type=jnp.float32,
        )
    chosen = jnp.where(owned, field, 0.0)
    for step in range(steps_own):
        mine = jnp.where(row_step == step, chosen, 0.0)
        out_ref[step : step + 1, :] = jnp.sum(mine, axis=0, keepdims=True).astype(out_ref.dtype)

    def drain(offset, carry):
        peer = lax.rem(me + offset, n_dev)
        out_copy(peer, me).wait_send()
        in_copy(peer, me).wait_send()
        return carry

    lax.fori_loop(1, n_dev, drain, 0)


def fused_body(
    n_dom,
    n_tm,
    panel_signal,
    panel_box,
    radiation,
    reception,
    translation,
    list_source,
    list_class,
    list_count,
):
    steps_own, panels = panel_signal.shape
    dirs_all = radiation.shape[1]
    classes, lags, _ = translation.shape
    boxes_all = list_source.shape[0]
    n_dev = n_dom * n_tm
    block = steps_own * (boxes_all // n_dom) // n_tm
    chunks = 4
    vmem = pl.BlockSpec(memory_space=pltpu.VMEM)
    smem = pl.BlockSpec(memory_space=pltpu.SMEM)
    hbm = pl.BlockSpec(memory_space=pl.ANY)
    message = pltpu.VMEM((n_dev, block, LANES), jnp.bfloat16)
    return pl.pallas_call(
        functools.partial(kernel, n_dom, n_tm),
        out_shape=jax.ShapeDtypeStruct((steps_own, panels), jnp.bfloat16),
        in_specs=[vmem, vmem, hbm, hbm, hbm, smem, smem, smem],
        out_specs=vmem,
        scratch_shapes=[
            pltpu.VMEM((panels, dirs_all), jnp.bfloat16),
            pltpu.VMEM((panels, dirs_all), jnp.bfloat16),
            pltpu.VMEM(translation.shape, jnp.bfloat16),
            pltpu.VMEM((classes * lags, LANES), jnp.float32),
            pltpu.VMEM((classes + 1, lags // n_tm, SUBLANES, LANES), jnp.float32),
            pltpu.VMEM((boxes_all, SUBLANES, LANES), jnp.float32),
            message,
            message,
            message,
            message,
            pltpu.VMEM((n_tm * block, LANES), jnp.float32),
            pltpu.SemaphoreType.DMA((2 * chunks + 2,)),
            pltpu.SemaphoreType.DMA((n_dev,)),
            pltpu.SemaphoreType.DMA((n_dev,)),
            pltpu.SemaphoreType.DMA((n_dev,)),
            pltpu.SemaphoreType.DMA((n_dev,)),
        ],
        compiler_params=pltpu.CompilerParams(collective_id=0, has_side_effects=True),
    )(
        panel_signal,
        panel_box.reshape(1, panels),
        radiation,
        reception,
        translation,
        list_source.T,
        list_class.T,
        list_count,
    )


def whole_body(n_dom, n_tm, *args):
    panel_signal, translation, boxes_all = args[0], args[4], args[5].shape[0]
    steps_own = panel_signal.shape[0]
    classes, lags, dirs_own = translation.shape
    boxes_own = boxes_all // n_dom
    fits = (
        dirs_own == LANES
        and LANES % n_tm == 0
        and lags == SUBLANES
        and steps_own * n_tm == lags
        and lags % n_tm == 0
        and boxes_own % n_tm == 0
        and steps_own * boxes_own == n_tm * SUBLANES
        and classes % SUBLANES == 0
    )
    if fits:
        return fused_body(n_dom, n_tm, *args)
    return body(*args)


def solution(mesh):
    placed = (
        P("tm", "dom"),
        P("dom"),
        P("dom", None),
        P("dom", None),
        P(None, None, "dom"),
        P(),
        P(),
        P(),
    )
    return jax.shard_map(
        functools.partial(whole_body, mesh.shape["dom"], mesh.shape["tm"]),
        mesh=mesh, in_specs=placed, out_specs=P("tm", "dom"), check_vma=False
    )
```

```python
import functools
import math

import jax
import jax.numpy as jnp
from jax import lax
from jax.experimental import pallas as pl
from jax.experimental.pallas import tpu as pltpu
from jax.sharding import PartitionSpec as P

def lag_sum(kern_rows, gathered, out_steps, offset):
    entries = kern_rows.shape[0]
    lags_all = kern_rows.shape[1]
    width = kern_rows.shape[2]
    results = []
    for step_out in range(out_steps):
        total = jnp.zeros((entries, width), jnp.float32)
        for step_in in range(gathered.shape[1]):
            delay = offset + step_out - step_in
            picked = lax.dynamic_index_in_dim(
                kern_rows, jnp.clip(delay, 0, lags_all - 1), 1, keepdims=False
            )
            weight = jnp.where(delay >= 0, picked.astype(jnp.float32), 0.0)
            total = total + weight * gathered[:, step_in].astype(jnp.float32)
        results.append(total)
    return jnp.stack(results, axis=1)


def body(
    panel_signal, panel_box, radiation, reception, translation, list_source, list_class, list_count
):
    rows_own = panel_signal.shape[0]
    dirs_own = translation.shape[2]
    boxes_all = list_source.shape[0]
    classes_all = translation.shape[0]
    lags_all = translation.shape[1]
    BOX_DEV = boxes_all // lax.axis_size("dom")
    J = list_source.shape[1]
    box_onehot = (panel_box[None, :] == jnp.arange(BOX_DEV, dtype=jnp.int32)[:, None]).astype(
        jnp.bfloat16
    )
    used_rows = (jnp.arange(J, dtype=jnp.int32)[None, :] < list_count[:, None]).astype(jnp.bfloat16)
    block_size = math.gcd(boxes_all, 256)

    def translate_all(table, rays, out_steps, offset):
        width = table.shape[2]
        count_in = rays.shape[1]
        flat_table = table.reshape(classes_all, lags_all * width)
        flat_rays = rays.reshape(boxes_all, count_in * width)

        def one_block(index):
            sources = lax.dynamic_slice_in_dim(
                list_source, index * block_size, block_size, 0
            ).reshape(block_size * J)
            classes = lax.dynamic_slice_in_dim(
                list_class, index * block_size, block_size, 0
            ).reshape(block_size * J)
            keep_rows = lax.dynamic_slice_in_dim(
                used_rows, index * block_size, block_size, 0
            ).reshape(block_size * J, 1)
            kern_rows = (jnp.take(flat_table, classes, axis=0) * keep_rows).reshape(
                block_size * J, lags_all, width
            )
            gathered = jnp.take(flat_rays, sources, axis=0).reshape(block_size * J, count_in, width)
            summed = lag_sum(kern_rows, gathered, out_steps, offset)
            return jnp.sum(summed.reshape(block_size, J, out_steps, width), axis=1)

        blocks = lax.map(one_block, jnp.arange(boxes_all // block_size, dtype=jnp.int32))
        return blocks.reshape(boxes_all, out_steps, width)

    masked = panel_signal[:, None, :] * box_onehot[None]
    outgoing = jnp.einsum(
        "rbp,pk->brk", masked, radiation, preferred_element_type=jnp.float32
    ).astype(jnp.bfloat16)
    spread = lax.all_to_all(outgoing, "dom", split_axis=2, concat_axis=0, tiled=True)
    first = lax.axis_index("tm") * rows_own
    empty = jnp.zeros((boxes_all, rows_own, dirs_own), jnp.float32)
    piece = lax.all_gather(spread, "tm", axis=1, tiled=True)

    def active():
        return empty + translate_all(translation, piece, rows_own, first)

    def passive():
        return empty

    incoming = lax.cond(jnp.int32(0) <= first + rows_own - 1, active, passive)
    rays = lax.all_to_all(
        incoming.astype(jnp.bfloat16), "dom", split_axis=0, concat_axis=2, tiled=True
    )
    partial_value = jnp.einsum("brk,pk->brp", rays, reception, preferred_element_type=jnp.float32)
    field = jnp.sum(partial_value * box_onehot.astype(jnp.float32)[:, None, :], axis=0)
    return field.astype(jnp.bfloat16)


LANES = 128
SUBLANES = 8
MESH = pl.DeviceIdType.MESH


def pick_lanes(parts, lane_group):
    total = parts[0]
    for index in range(1, len(parts)):
        total = jnp.where(lane_group == index, parts[index], total)
    return total


def spin(values, shift):
    shift = shift % LANES
    return values if shift == 0 else pltpu.roll(values, shift, 1)


def partner(mine, step, count):
    if count & (count - 1):
        return lax.rem(mine + step, count)
    total, bit = mine, 1
    while bit < count:
        turn = (step // bit) % 2 if isinstance(step, int) else lax.rem(lax.div(step, bit), 2)
        if not isinstance(turn, int) or turn:
            total = total + turn * bit * (1 - 2 * lax.rem(lax.div(mine, bit), 2))
        bit *= 2
    return total


def kernel(
    n_dom,
    n_tm,
    signal_ref,
    box_ref,
    rad_hbm,
    rec_hbm,
    trans_hbm,
    source_ref,
    class_ref,
    count_ref,
    out_ref,
    rad,
    rec,
    trans,
    trans_wide,
    kern,
    rays,
    send_out,
    recv_out,
    send_in,
    recv_in,
    rows_tmp,
    load_sem,
    out_send_sem,
    out_recv_sem,
    in_send_sem,
    in_recv_sem,
):
    n_dev = n_dom * n_tm
    dom, tm = lax.axis_index("dom"), lax.axis_index("tm")
    me = dom * n_tm + tm
    steps_own, panels = signal_ref.shape
    dirs_all = rad.shape[1]
    classes, lags, _ = trans.shape
    entries = source_ref.shape[0]
    boxes_own = source_ref.shape[1] // n_dom
    span = LANES // n_tm
    pieces = boxes_own // n_tm
    block = steps_own * pieces
    rows_all = n_tm * block
    halves = lags // n_tm
    chunks = load_sem.shape[0] // 2 - 1
    depth = panels // chunks

    def place(peer):
        return {"dom": lax.div(peer, n_tm), "tm": lax.rem(peer, n_tm)}

    def rad_copy(index):
        at = pl.ds(index * depth, depth)
        return pltpu.make_async_copy(rad_hbm.at[at, :], rad.at[at, :], load_sem.at[index])

    rec_copy = pltpu.make_async_copy(rec_hbm, rec, load_sem.at[chunks])
    trans_copy = pltpu.make_async_copy(trans_hbm, trans, load_sem.at[chunks + 1])

    for index in range(chunks):
        rad_copy(index).start()
    trans_copy.start()
    rec_copy.start()

    barrier = pltpu.get_barrier_semaphore()

    def greet(offset, carry):
        peer = lax.rem(me + offset, n_dev)
        pl.semaphore_signal(barrier, inc=1, device_id=place(peer), device_id_type=MESH)
        return carry

    lax.fori_loop(1, n_dev, greet, 0)

    lane_group = lax.broadcasted_iota(jnp.int32, (SUBLANES, LANES), 1) // span
    sublane = lax.broadcasted_iota(jnp.int32, (SUBLANES, LANES), 0)

    row = lax.broadcasted_iota(jnp.int32, (rows_all, panels), 0)
    row_box = (row % pieces) * n_tm + row // block
    owned = box_ref[...] == row_box
    signal = signal_ref[...].astype(jnp.float32)
    spread = signal[0:1]
    row_step = (row // pieces) % steps_own
    for step in range(1, steps_own):
        spread = jnp.where(row_step == step, signal[step : step + 1], spread)
    masked = jnp.where(owned, spread, 0.0).astype(jnp.bfloat16)

    outgoing = jnp.zeros((rows_all, dirs_all), jnp.float32)
    for index in range(chunks):
        rad_copy(index).wait()
        outgoing = outgoing + jnp.dot(
            masked[:, index * depth : (index + 1) * depth],
            rad[index * depth : (index + 1) * depth, :],
            preferred_element_type=jnp.float32,
        )
    for owner in range(n_dom):
        tiles = [
            outgoing[part * block : (part + 1) * block, owner * LANES : (owner + 1) * LANES]
            for part in range(n_tm)
        ]
        for time in range(n_tm):
            moved = [spin(tiles[part], span * (part - time)) for part in range(n_tm)]
            send_out[owner * n_tm + time] = pick_lanes(moved, lane_group).astype(jnp.bfloat16)

    trans_copy.wait()
    trans_wide[...] = trans[...].astype(jnp.float32).reshape(classes * lags, LANES)
    kern[classes] = jnp.zeros((halves, SUBLANES, LANES), jnp.float32)

    def spread_class(index, carry):
        base = index * (SUBLANES * lags)
        for half in range(halves):
            moved = []
            for part in range(n_tm):
                tile = trans_wide[pl.ds(base + half * n_tm + part, SUBLANES, stride=lags), :]
                shift = lax.rem((part - tm + n_tm) * span, LANES)
                moved.append(pltpu.roll(tile, shift, 1))
            tile = pick_lanes(moved, lane_group)
            for at in range(SUBLANES):
                kern[index * SUBLANES + at, half] = jnp.broadcast_to(
                    tile[at : at + 1], (SUBLANES, LANES)
                )
        return carry

    lax.fori_loop(0, classes // SUBLANES, spread_class, 0)

    pl.semaphore_wait(barrier, n_dev - 1)

    def out_copy(peer, slot):
        return pltpu.make_async_remote_copy(
            src_ref=send_out.at[peer],
            dst_ref=recv_out.at[slot],
            send_sem=out_send_sem.at[peer],
            recv_sem=out_recv_sem.at[slot],
            device_id=place(peer),
            device_id_type=MESH,
        )

    def in_copy(peer, slot):
        return pltpu.make_async_remote_copy(
            src_ref=send_in.at[peer],
            dst_ref=recv_in.at[slot],
            send_sem=in_send_sem.at[peer],
            recv_sem=in_recv_sem.at[slot],
            device_id=place(peer),
            device_id_type=MESH,
        )

    def send_first(offset, carry):
        out_copy(partner(me, n_dev - offset, n_dev), me).start()
        return carry

    lax.fori_loop(1, n_dev, send_first, 0)
    recv_out[me] = send_out[me]

    def take_rays(step, carry):
        owner = partner(dom, step, n_dom)
        for time in range(n_tm):
            slot = owner * n_tm + time

            @pl.when(slot != me)
            def _():
                out_copy(slot, slot).wait_recv()

            rows_tmp[time * block : (time + 1) * block, :] = recv_out[slot].astype(jnp.float32)
        for piece in range(pieces):
            tile = rows_tmp[pl.ds(piece, SUBLANES, stride=pieces), :]
            later = [tile]
            for lag in range(1, n_tm):
                later.append(jnp.where(sublane >= lag, pltpu.roll(tile, lag, 0), 0.0))
            for part in range(n_tm):
                moved = [spin(later[lag], span * (lag - part)) for lag in range(n_tm)]
                rays[owner * boxes_own + piece * n_tm + part] = pick_lanes(moved, lane_group)
        return carry

    lax.fori_loop(0, n_dom, take_rays, 0)

    def translate(step, carry):
        owner = partner(dom, n_dom - 1 - step, n_dom)
        for piece in range(pieces):
            sums = []
            for part in range(n_tm):
                box = owner * boxes_own + piece * n_tm + part
                used = count_ref[box]
                totals = [jnp.zeros((SUBLANES, LANES), jnp.float32) for _ in range(halves)]
                for entry in range(entries):
                    kind = jnp.where(entry < used, class_ref[entry, box], classes)
                    ray = rays[source_ref[entry, box]]
                    for half in range(halves):
                        totals[half] = totals[half] + kern[kind, half] * ray
                total = totals[0]
                for half in range(1, halves):
                    late = half * n_tm
                    total = total + jnp.where(
                        sublane >= late, pltpu.roll(totals[half], late, 0), 0.0
                    )
                sums.append(total)
            width = n_tm
            while width > 1:
                width //= 2
                near = (lane_group // width) % 2 == 0
                sums = [
                    jnp.where(near, sums[part], sums[part + width])
                    + pltpu.roll(
                        jnp.where(near, sums[part + width], sums[part]), width * span, 1
                    )
                    if width * 2 * span == LANES
                    else jnp.where(near, sums[part], sums[part + width])
                    + jnp.where(
                        near,
                        pltpu.roll(sums[part], LANES - width * span, 1),
                        pltpu.roll(sums[part + width], width * span, 1),
                    )
                    for part in range(width)
                ]
            rows_tmp[pl.ds(piece, SUBLANES, stride=pieces), :] = sums[0]
        for time in range(n_tm):
            slot = owner * n_tm + time
            send_in[slot] = rows_tmp[time * block : (time + 1) * block, :].astype(jnp.bfloat16)

            @pl.when(slot != me)
            def _():
                in_copy(slot, me).start()

        return carry

    lax.fori_loop(0, n_dom, translate, 0)
    recv_in[me] = send_in[me]

    rec_copy.wait()
    field = jnp.zeros((rows_all, panels), jnp.float32)
    for step in range(n_dom):
        owner = partner(dom, n_dom - 1 - step, n_dom)
        tiles = []
        for time in range(n_tm):
            slot = owner * n_tm + time

            @pl.when(slot != me)
            def _():
                in_copy(slot, slot).wait_recv()

            tiles.append(recv_in[slot].astype(jnp.float32))
        incoming = []
        for part in range(n_tm):
            moved = [spin(tiles[time], span * (time - part)) for time in range(n_tm)]
            incoming.append(pick_lanes(moved, lane_group))
        incoming = jnp.concatenate(incoming, axis=0).astype(jnp.bfloat16)
        field = field + lax.dot_general(
            incoming,
            rec[:, pl.ds(pl.multiple_of(owner * LANES, LANES), LANES)],
            (((1,), (1,)), ((), ())),
            preferred_element_type=jnp.float32,
        )
    chosen = jnp.where(owned, field, 0.0)
    for step in range(steps_own):
        mine = jnp.where(row_step == step, chosen, 0.0)
        out_ref[step : step + 1, :] = jnp.sum(mine, axis=0, keepdims=True).astype(out_ref.dtype)

    def drain(offset, carry):
        peer = lax.rem(me + offset, n_dev)
        out_copy(peer, me).wait_send()
        in_copy(peer, me).wait_send()
        return carry

    lax.fori_loop(1, n_dev, drain, 0)


def fused_body(
    n_dom,
    n_tm,
    panel_signal,
    panel_box,
    radiation,
    reception,
    translation,
    list_source,
    list_class,
    list_count,
):
    steps_own, panels = panel_signal.shape
    dirs_all = radiation.shape[1]
    classes, lags, _ = translation.shape
    boxes_all = list_source.shape[0]
    n_dev = n_dom * n_tm
    block = steps_own * (boxes_all // n_dom) // n_tm
    chunks = 4
    vmem = pl.BlockSpec(memory_space=pltpu.VMEM)
    smem = pl.BlockSpec(memory_space=pltpu.SMEM)
    hbm = pl.BlockSpec(memory_space=pl.ANY)
    message = pltpu.VMEM((n_dev, block, LANES), jnp.bfloat16)
    return pl.pallas_call(
        functools.partial(kernel, n_dom, n_tm),
        out_shape=jax.ShapeDtypeStruct((steps_own, panels), jnp.bfloat16),
        in_specs=[vmem, vmem, hbm, hbm, hbm, smem, smem, smem],
        out_specs=vmem,
        scratch_shapes=[
            pltpu.VMEM((panels, dirs_all), jnp.bfloat16),
            pltpu.VMEM((panels, dirs_all), jnp.bfloat16),
            pltpu.VMEM(translation.shape, jnp.bfloat16),
            pltpu.VMEM((classes * lags, LANES), jnp.float32),
            pltpu.VMEM((classes + 1, lags // n_tm, SUBLANES, LANES), jnp.float32),
            pltpu.VMEM((boxes_all, SUBLANES, LANES), jnp.float32),
            message,
            message,
            message,
            message,
            pltpu.VMEM((n_tm * block, LANES), jnp.float32),
            pltpu.SemaphoreType.DMA((2 * chunks + 2,)),
            pltpu.SemaphoreType.DMA((n_dev,)),
            pltpu.SemaphoreType.DMA((n_dev,)),
            pltpu.SemaphoreType.DMA((n_dev,)),
            pltpu.SemaphoreType.DMA((n_dev,)),
        ],
        compiler_params=pltpu.CompilerParams(collective_id=0, has_side_effects=True),
    )(
        panel_signal,
        panel_box.reshape(1, panels),
        radiation,
        reception,
        translation,
        list_source.T,
        list_class.T,
        list_count,
    )


def whole_body(n_dom, n_tm, *args):
    panel_signal, translation, boxes_all = args[0], args[4], args[5].shape[0]
    steps_own = panel_signal.shape[0]
    classes, lags, dirs_own = translation.shape
    boxes_own = boxes_all // n_dom
    fits = (
        dirs_own == LANES
        and LANES % n_tm == 0
        and lags == SUBLANES
        and steps_own * n_tm == lags
        and lags % n_tm == 0
        and boxes_own % n_tm == 0
        and steps_own * boxes_own == n_tm * SUBLANES
        and classes % SUBLANES == 0
    )
    if fits:
        return fused_body(n_dom, n_tm, *args)
    return body(*args)


def solution(mesh):
    placed = (
        P("tm", "dom"),
        P("dom"),
        P("dom", None),
        P("dom", None),
        P(None, None, "dom"),
        P(),
        P(),
        P(),
    )
    return jax.shard_map(
        functools.partial(whole_body, mesh.shape["dom"], mesh.shape["tm"]),
        mesh=mesh, in_specs=placed, out_specs=P("tm", "dom"), check_vma=False
    )
```

```python
import functools
import math

import jax
import jax.numpy as jnp
from jax import lax
from jax.experimental import pallas as pl
from jax.experimental.pallas import tpu as pltpu
from jax.sharding import PartitionSpec as P

def lag_sum(kern_rows, gathered, out_steps, offset):
    entries = kern_rows.shape[0]
    lags_all = kern_rows.shape[1]
    width = kern_rows.shape[2]
    results = []
    for step_out in range(out_steps):
        total = jnp.zeros((entries, width), jnp.float32)
        for step_in in range(gathered.shape[1]):
            delay = offset + step_out - step_in
            picked = lax.dynamic_index_in_dim(
                kern_rows, jnp.clip(delay, 0, lags_all - 1), 1, keepdims=False
            )
            weight = jnp.where(delay >= 0, picked.astype(jnp.float32), 0.0)
            total = total + weight * gathered[:, step_in].astype(jnp.float32)
        results.append(total)
    return jnp.stack(results, axis=1)


def body(
    panel_signal, panel_box, radiation, reception, translation, list_source, list_class, list_count
):
    rows_own = panel_signal.shape[0]
    dirs_own = translation.shape[2]
    boxes_all = list_source.shape[0]
    classes_all = translation.shape[0]
    lags_all = translation.shape[1]
    BOX_DEV = boxes_all // lax.axis_size("dom")
    J = list_source.shape[1]
    box_onehot = (panel_box[None, :] == jnp.arange(BOX_DEV, dtype=jnp.int32)[:, None]).astype(
        jnp.bfloat16
    )
    used_rows = (jnp.arange(J, dtype=jnp.int32)[None, :] < list_count[:, None]).astype(jnp.bfloat16)
    block_size = math.gcd(boxes_all, 256)

    def translate_all(table, rays, out_steps, offset):
        width = table.shape[2]
        count_in = rays.shape[1]
        flat_table = table.reshape(classes_all, lags_all * width)
        flat_rays = rays.reshape(boxes_all, count_in * width)

        def one_block(index):
            sources = lax.dynamic_slice_in_dim(
                list_source, index * block_size, block_size, 0
            ).reshape(block_size * J)
            classes = lax.dynamic_slice_in_dim(
                list_class, index * block_size, block_size, 0
            ).reshape(block_size * J)
            keep_rows = lax.dynamic_slice_in_dim(
                used_rows, index * block_size, block_size, 0
            ).reshape(block_size * J, 1)
            kern_rows = (jnp.take(flat_table, classes, axis=0) * keep_rows).reshape(
                block_size * J, lags_all, width
            )
            gathered = jnp.take(flat_rays, sources, axis=0).reshape(block_size * J, count_in, width)
            summed = lag_sum(kern_rows, gathered, out_steps, offset)
            return jnp.sum(summed.reshape(block_size, J, out_steps, width), axis=1)

        blocks = lax.map(one_block, jnp.arange(boxes_all // block_size, dtype=jnp.int32))
        return blocks.reshape(boxes_all, out_steps, width)

    masked = panel_signal[:, None, :] * box_onehot[None]
    outgoing = jnp.einsum(
        "rbp,pk->brk", masked, radiation, preferred_element_type=jnp.float32
    ).astype(jnp.bfloat16)
    spread = lax.all_to_all(outgoing, "dom", split_axis=2, concat_axis=0, tiled=True)
    first = lax.axis_index("tm") * rows_own
    empty = jnp.zeros((boxes_all, rows_own, dirs_own), jnp.float32)
    piece = lax.all_gather(spread, "tm", axis=1, tiled=True)

    def active():
        return empty + translate_all(translation, piece, rows_own, first)

    def passive():
        return empty

    incoming = lax.cond(jnp.int32(0) <= first + rows_own - 1, active, passive)
    rays = lax.all_to_all(
        incoming.astype(jnp.bfloat16), "dom", split_axis=0, concat_axis=2, tiled=True
    )
    partial_value = jnp.einsum("brk,pk->brp", rays, reception, preferred_element_type=jnp.float32)
    field = jnp.sum(partial_value * box_onehot.astype(jnp.float32)[:, None, :], axis=0)
    return field.astype(jnp.bfloat16)


LANES = 128
SUBLANES = 8
MESH = pl.DeviceIdType.MESH


def pick_lanes(parts, lane_group):
    total = parts[0]
    for index in range(1, len(parts)):
        total = jnp.where(lane_group == index, parts[index], total)
    return total


def spin(values, shift):
    shift = shift % LANES
    return values if shift == 0 else pltpu.roll(values, shift, 1)


def partner(mine, step, count):
    if count & (count - 1):
        return lax.rem(mine + step, count)
    total, bit = mine, 1
    while bit < count:
        turn = (step // bit) % 2 if isinstance(step, int) else lax.rem(lax.div(step, bit), 2)
        if not isinstance(turn, int) or turn:
            total = total + turn * bit * (1 - 2 * lax.rem(lax.div(mine, bit), 2))
        bit *= 2
    return total


def kernel(
    n_dom,
    n_tm,
    signal_hbm,
    box_hbm,
    rad_hbm,
    rec_hbm,
    trans_hbm,
    source_hbm,
    class_hbm,
    count_hbm,
    out_ref,
    signal_ref,
    box_ref,
    source_ref,
    class_ref,
    count_ref,
    small_sem,
    rad,
    rec,
    trans,
    trans_wide,
    kern,
    rays,
    send_out,
    recv_out,
    send_in,
    recv_in,
    rows_tmp,
    load_sem,
    out_send_sem,
    out_recv_sem,
    in_send_sem,
    in_recv_sem,
):
    n_dev = n_dom * n_tm
    dom, tm = lax.axis_index("dom"), lax.axis_index("tm")
    me = dom * n_tm + tm
    steps_own, panels = signal_ref.shape
    dirs_all = rad.shape[1]
    classes, lags, _ = trans.shape
    entries = source_ref.shape[0]
    boxes_own = source_ref.shape[1] // n_dom
    span = LANES // n_tm
    pieces = boxes_own // n_tm
    block = steps_own * pieces
    rows_all = n_tm * block
    halves = lags // n_tm
    chunks = load_sem.shape[0] // 2 - 1
    depth = panels // chunks

    def place(peer):
        return {"dom": lax.div(peer, n_tm), "tm": lax.rem(peer, n_tm)}

    def rad_copy(index):
        at = pl.ds(index * depth, depth)
        return pltpu.make_async_copy(rad_hbm.at[at, :], rad.at[at, :], load_sem.at[index])

    rec_copy = pltpu.make_async_copy(rec_hbm, rec, load_sem.at[chunks])
    trans_copy = pltpu.make_async_copy(trans_hbm, trans, load_sem.at[chunks + 1])

    barrier = pltpu.get_barrier_semaphore()

    def greet(offset, carry):
        peer = partner(me, n_dev - offset, n_dev)
        pl.semaphore_signal(barrier, inc=1, device_id=place(peer), device_id_type=MESH)
        return carry

    small = [
        pltpu.make_async_copy(source, target, small_sem.at[index])
        for index, (source, target) in enumerate(
            [
                (signal_hbm, signal_ref),
                (box_hbm, box_ref),
                (source_hbm, source_ref),
                (class_hbm, class_ref),
                (count_hbm, count_ref),
            ]
        )
    ]
    small[0].start()
    small[1].start()
    for index in range(chunks):
        rad_copy(index).start()
    lax.fori_loop(1, n_dev, greet, 0)
    trans_copy.start()
    for copy in small[2:]:
        copy.start()
    rec_copy.start()
    small[0].wait()
    small[1].wait()

    lane_group = lax.broadcasted_iota(jnp.int32, (SUBLANES, LANES), 1) // span
    sublane = lax.broadcasted_iota(jnp.int32, (SUBLANES, LANES), 0)

    row = lax.broadcasted_iota(jnp.int32, (rows_all, panels), 0)
    row_box = (row % pieces) * n_tm + row // block
    owned = box_ref[...] == row_box
    signal = signal_ref[...].astype(jnp.float32)
    spread = signal[0:1]
    row_step = (row // pieces) % steps_own
    for step in range(1, steps_own):
        spread = jnp.where(row_step == step, signal[step : step + 1], spread)
    masked = jnp.where(owned, spread, 0.0).astype(jnp.bfloat16)

    outgoing = jnp.zeros((rows_all, dirs_all), jnp.float32)
    for index in range(chunks):
        rad_copy(index).wait()
        outgoing = outgoing + jnp.dot(
            masked[:, index * depth : (index + 1) * depth],
            rad[index * depth : (index + 1) * depth, :],
            preferred_element_type=jnp.float32,
        )
    for owner in range(n_dom):
        tiles = [
            outgoing[part * block : (part + 1) * block, owner * LANES : (owner + 1) * LANES]
            for part in range(n_tm)
        ]
        for time in range(n_tm):
            moved = [spin(tiles[part], span * (part - time)) for part in range(n_tm)]
            send_out[owner * n_tm + time] = pick_lanes(moved, lane_group).astype(jnp.bfloat16)

    trans_copy.wait()
    trans_wide[...] = trans[...].astype(jnp.float32).reshape(classes * lags, LANES)
    kern[classes] = jnp.zeros((halves, SUBLANES, LANES), jnp.float32)

    def spread_class(index, carry):
        base = index * (SUBLANES * lags)
        for half in range(halves):
            moved = []
            for part in range(n_tm):
                tile = trans_wide[pl.ds(base + half * n_tm + part, SUBLANES, stride=lags), :]
                shift = lax.rem((part - tm + n_tm) * span, LANES)
                moved.append(pltpu.roll(tile, shift, 1))
            tile = pick_lanes(moved, lane_group)
            for at in range(SUBLANES):
                kern[index * SUBLANES + at, half] = jnp.broadcast_to(
                    tile[at : at + 1], (SUBLANES, LANES)
                )
        return carry

    lax.fori_loop(0, classes // SUBLANES, spread_class, 0)

    pl.semaphore_wait(barrier, n_dev - 1)

    def out_copy(peer, slot):
        return pltpu.make_async_remote_copy(
            src_ref=send_out.at[peer],
            dst_ref=recv_out.at[slot],
            send_sem=out_send_sem.at[peer],
            recv_sem=out_recv_sem.at[slot],
            device_id=place(peer),
            device_id_type=MESH,
        )

    def in_copy(peer, slot):
        return pltpu.make_async_remote_copy(
            src_ref=send_in.at[peer],
            dst_ref=recv_in.at[slot],
            send_sem=in_send_sem.at[peer],
            recv_sem=in_recv_sem.at[slot],
            device_id=place(peer),
            device_id_type=MESH,
        )

    def send_first(offset, carry):
        out_copy(partner(me, n_dev - offset, n_dev), me).start()
        return carry

    lax.fori_loop(1, n_dev, send_first, 0)
    recv_out[me] = send_out[me]

    def take_rays(step, carry):
        owner = partner(dom, step, n_dom)
        for time in range(n_tm):
            slot = owner * n_tm + time

            @pl.when(slot != me)
            def _():
                out_copy(slot, slot).wait_recv()

            rows_tmp[time * block : (time + 1) * block, :] = recv_out[slot].astype(jnp.float32)
        for piece in range(pieces):
            tile = rows_tmp[pl.ds(piece, SUBLANES, stride=pieces), :]
            later = [tile]
            for lag in range(1, n_tm):
                later.append(jnp.where(sublane >= lag, pltpu.roll(tile, lag, 0), 0.0))
            for part in range(n_tm):
                moved = [spin(later[lag], span * (lag - part)) for lag in range(n_tm)]
                rays[owner * boxes_own + piece * n_tm + part] = pick_lanes(moved, lane_group)
        return carry

    for step in range(n_dom):
        take_rays(step, 0)
    for copy in small[2:]:
        copy.wait()

    def translate(step, carry):
        owner = partner(dom, n_dom - 1 - step, n_dom)
        for piece in range(pieces):
            sums = []
            for part in range(n_tm):
                box = owner * boxes_own + piece * n_tm + part
                used = count_ref[box]
                totals = [jnp.zeros((SUBLANES, LANES), jnp.float32) for _ in range(halves)]
                for entry in range(entries):
                    kind = jnp.where(entry < used, class_ref[entry, box], classes)
                    ray = rays[source_ref[entry, box]]
                    for half in range(halves):
                        totals[half] = totals[half] + kern[kind, half] * ray
                total = totals[0]
                for half in range(1, halves):
                    late = half * n_tm
                    total = total + jnp.where(
                        sublane >= late, pltpu.roll(totals[half], late, 0), 0.0
                    )
                sums.append(total)
            width = n_tm
            while width > 1:
                width //= 2
                near = (lane_group // width) % 2 == 0
                sums = [
                    jnp.where(near, sums[part], sums[part + width])
                    + pltpu.roll(
                        jnp.where(near, sums[part + width], sums[part]), width * span, 1
                    )
                    if width * 2 * span == LANES
                    else jnp.where(near, sums[part], sums[part + width])
                    + jnp.where(
                        near,
                        pltpu.roll(sums[part], LANES - width * span, 1),
                        pltpu.roll(sums[part + width], width * span, 1),
                    )
                    for part in range(width)
                ]
            rows_tmp[pl.ds(piece, SUBLANES, stride=pieces), :] = sums[0]
        for time in range(n_tm):
            slot = owner * n_tm + time
            send_in[slot] = rows_tmp[time * block : (time + 1) * block, :].astype(jnp.bfloat16)

            @pl.when(slot != me)
            def _():
                in_copy(slot, me).start()

        return carry

    lax.fori_loop(0, n_dom, translate, 0)
    recv_in[me] = send_in[me]

    rec_copy.wait()
    field = jnp.zeros((rows_all, panels), jnp.float32)
    for step in range(n_dom):
        owner = partner(dom, n_dom - 1 - step, n_dom)
        tiles = []
        for time in range(n_tm):
            slot = owner * n_tm + time

            @pl.when(slot != me)
            def _():
                in_copy(slot, slot).wait_recv()

            tiles.append(recv_in[slot].astype(jnp.float32))
        incoming = []
        for part in range(n_tm):
            moved = [spin(tiles[time], span * (time - part)) for time in range(n_tm)]
            incoming.append(pick_lanes(moved, lane_group))
        incoming = jnp.concatenate(incoming, axis=0).astype(jnp.bfloat16)
        field = field + lax.dot_general(
            incoming,
            rec[:, pl.ds(pl.multiple_of(owner * LANES, LANES), LANES)],
            (((1,), (1,)), ((), ())),
            preferred_element_type=jnp.float32,
        )
    chosen = jnp.where(owned, field, 0.0)
    for step in range(steps_own):
        mine = jnp.where(row_step == step, chosen, 0.0)
        out_ref[step : step + 1, :] = jnp.sum(mine, axis=0, keepdims=True).astype(out_ref.dtype)

    def drain(offset, carry):
        peer = lax.rem(me + offset, n_dev)
        out_copy(peer, me).wait_send()
        in_copy(peer, me).wait_send()
        return carry

    lax.fori_loop(1, n_dev, drain, 0)


def fused_body(
    n_dom,
    n_tm,
    panel_signal,
    panel_box,
    radiation,
    reception,
    translation,
    list_source,
    list_class,
    list_count,
):
    steps_own, panels = panel_signal.shape
    dirs_all = radiation.shape[1]
    classes, lags, _ = translation.shape
    boxes_all = list_source.shape[0]
    n_dev = n_dom * n_tm
    block = steps_own * (boxes_all // n_dom) // n_tm
    chunks = 4
    vmem = pl.BlockSpec(memory_space=pltpu.VMEM)
    hbm = pl.BlockSpec(memory_space=pl.ANY)
    message = pltpu.VMEM((n_dev, block, LANES), jnp.bfloat16)
    return pl.pallas_call(
        functools.partial(kernel, n_dom, n_tm),
        out_shape=jax.ShapeDtypeStruct((steps_own, panels), jnp.bfloat16),
        in_specs=[hbm] * 8,
        out_specs=vmem,
        scratch_shapes=[
            pltpu.VMEM((steps_own, panels), jnp.bfloat16),
            pltpu.VMEM((1, panels), jnp.int32),
            pltpu.SMEM(list_source.shape[::-1], jnp.int32),
            pltpu.SMEM(list_class.shape[::-1], jnp.int32),
            pltpu.SMEM(list_count.shape, jnp.int32),
            pltpu.SemaphoreType.DMA((5,)),
            pltpu.VMEM((panels, dirs_all), jnp.bfloat16),
            pltpu.VMEM((panels, dirs_all), jnp.bfloat16),
            pltpu.VMEM(translation.shape, jnp.bfloat16),
            pltpu.VMEM((classes * lags, LANES), jnp.float32),
            pltpu.VMEM((classes + 1, lags // n_tm, SUBLANES, LANES), jnp.float32),
            pltpu.VMEM((boxes_all, SUBLANES, LANES), jnp.float32),
            message,
            message,
            message,
            message,
            pltpu.VMEM((n_tm * block, LANES), jnp.float32),
            pltpu.SemaphoreType.DMA((2 * chunks + 2,)),
            pltpu.SemaphoreType.DMA((n_dev,)),
            pltpu.SemaphoreType.DMA((n_dev,)),
            pltpu.SemaphoreType.DMA((n_dev,)),
            pltpu.SemaphoreType.DMA((n_dev,)),
        ],
        compiler_params=pltpu.CompilerParams(collective_id=0, has_side_effects=True),
    )(
        panel_signal,
        panel_box.reshape(1, panels),
        radiation,
        reception,
        translation,
        list_source.T,
        list_class.T,
        list_count,
    )


def whole_body(n_dom, n_tm, *args):
    panel_signal, translation, boxes_all = args[0], args[4], args[5].shape[0]
    steps_own = panel_signal.shape[0]
    classes, lags, dirs_own = translation.shape
    boxes_own = boxes_all // n_dom
    fits = (
        dirs_own == LANES
        and LANES % n_tm == 0
        and lags == SUBLANES
        and steps_own * n_tm == lags
        and lags % n_tm == 0
        and boxes_own % n_tm == 0
        and steps_own * boxes_own == n_tm * SUBLANES
        and classes % SUBLANES == 0
    )
    if fits:
        return fused_body(n_dom, n_tm, *args)
    return body(*args)


def solution(mesh):
    placed = (
        P("tm", "dom"),
        P("dom"),
        P("dom", None),
        P("dom", None),
        P(None, None, "dom"),
        P(),
        P(),
        P(),
    )
    return jax.shard_map(
        functools.partial(whole_body, mesh.shape["dom"], mesh.shape["tm"]),
        mesh=mesh, in_specs=placed, out_specs=P("tm", "dom"), check_vma=False
    )
```
